128 devices in a mesh: tm: 32 (over z, x_lo, y), head: 4 (over x_hi, core).
Axes of the slice: x: 4 (x_hi: 2, x_lo: 2; x = x_hi * 2 + x_lo), y: 4, z: 4, core: 2. Of those that a mesh axis runs over, the one named last changes fastest.
Arguments:
- queries: bfloat16 [32768, 1024], P('tm', 'head'), may hold values from -8 to 8
- keys: bfloat16 [32768, 1024], P('tm', 'head'), may hold values from -8 to 8
- values: bfloat16 [32768, 1024], P('tm', 'head'), may hold values from -6 to 6
- out_weight: bfloat16 [1024, 1024], P('head'), may hold values from -0.1875 to 0.1875
- grad_output: bfloat16 [32768, 1024], P('tm'), may hold values from -6 to 6
- tile_lists: int32 [256, 5], P('tm'), may hold values from -1 to 255, as said below
Outputs:
- output: bfloat16 [32768, 1024], P('tm', 'head')
- grad_queries: bfloat16 [32768, 1024], P('tm', 'head')
- grad_keys: bfloat16 [32768, 1024], P('tm', 'head')
- grad_values: bfloat16 [32768, 1024], P('tm', 'head')
- grad_weight: float32 [1024, 1024], P('head', 'tm')
The draws below stay inside these ranges and needn't reach their ends.
Inputs may be any that keep to these rules, and one draw needn't show every extreme that they name: `tile_lists`: the row of query tile b lists distinct key tiles t of b's recording session with b - 4 <= t <= b in falling order, the first entry b itself, then -1 in unused slots; the first tile of every stretch but the first lists the tile before it; in every draw some row uses all 5 slots.
All inputs are finite; a program needn't handle non-finite values.
Results may differ from the reference program's by a relative error of at most 0.0095.
Values may be sent and summed in bfloat16 or wider, within the bound.
No kernel may reach another device: no remote copies, remote signals or barrier semaphores. Data moves between devices by JAX's collectives and lax.ppermute only.
A program may use at most 128 MiB of HBM per device.

```python
import jax
import jax.numpy as jnp
from jax import lax

D = 1024
HEADS = 16
HD = 64
QB = 128
TOK_DEV = 1024
STRETCH = 512
CT = 4
TOKENS = 32768
N_TM = 32


def base_field(key, salt):
    subkey = jax.random.fold_in(key, salt)
    return jnp.clip(jax.random.normal(subkey, (TOKENS, D)), -6.0, 6.0)


def draw_queries(key, part):
    field = base_field(key, 11)
    return field.astype(jnp.bfloat16)


def draw_keys(key, part):
    field = base_field(key, 12)
    return field.astype(jnp.bfloat16)


def draw_tile_lists(key, part):
    blocks = TOKENS // QB
    per_piece = TOK_DEV // (2 * QB)
    reach_tiles = per_piece + 1
    devices = TOKENS // TOK_DEV
    position = jnp.arange(blocks, dtype=jnp.int32)
    piece_start = (position % per_piece == 0) & (position > 0)
    boundary = jax.random.randint(jax.random.fold_in(key, 41), (blocks,), 0, 2 * per_piece + 1) == 0
    anchor = jax.random.randint(jax.random.fold_in(key, 42), (), per_piece, blocks)
    boundary = boundary & jnp.logical_not((position > anchor - per_piece) & (position <= anchor))
    boundary = boundary & jnp.logical_not(piece_start)
    boundary = boundary | (position == 0)
    session_start = lax.cummax(jnp.where(boundary, position, 0), axis=0)
    lag_index = jnp.arange(reach_tiles, dtype=jnp.int32)
    candidate = position[:, None] - lag_index[None, :]
    kept_slot = jax.random.randint(jax.random.fold_in(key, 43), (blocks, reach_tiles), 0, 4) != 0
    kept_slot = kept_slot | (lag_index[None, :] == 0) | (position[:, None] == anchor)
    kept_slot = kept_slot | (lag_index[None, :] == 1) & piece_start[:, None]
    live_slot = kept_slot & (candidate >= session_start[:, None])
    order_key = jnp.where(live_slot, lag_index[None, :], reach_tiles + lag_index[None, :])
    slot_order = jnp.argsort(order_key, axis=1, stable=True)
    listed = jnp.take_along_axis(jnp.where(live_slot, candidate, -1), slot_order, axis=1)
    ordered = listed.reshape(2 * devices, per_piece, reach_tiles)
    stored = jnp.stack([ordered[:devices], ordered[devices:][::-1]], axis=1)
    return stored.reshape(blocks, reach_tiles).astype(jnp.int32)


def spiked(drawn, rng, source, target, blocks, factor):
    owner, partner = [(jnp.arange(drawn.shape[axis_at]) // (drawn.shape[axis_at] // blocks)).reshape([-1 if axis == axis_at else 1 for axis in range(drawn.ndim)]) for axis_at in (source, target)]
    chosen = jax.random.permutation(rng, blocks)[partner]
    strong = (owner == chosen) | (owner == (partner + blocks // 2) % blocks)
    return jnp.where(strong, factor * drawn, drawn)


def level_of(own_key, extent, cuts, smallest, largest):
    loudness = 1.0
    for dim, shards_of in cuts:
        steps = jax.random.uniform(jax.random.fold_in(jax.random.fold_in(own_key, 6), dim), (shards_of,), jnp.float32, smallest / len(cuts), largest / len(cuts))
        loudness = loudness * jnp.repeat(jnp.exp(steps), extent[dim] // shards_of).reshape((-1,) + (1,) * (len(extent) - 1 - dim))
    return loudness


def scatter_about(own_key, shape, width, bound, cuts=(), held_as=jnp.bfloat16):
    result = width * jax.random.normal(own_key, shape, jnp.float32)
    if cuts:
        result = result * level_of(own_key, shape, cuts, -0.22, 0.18)
    return jnp.clip(result, -bound, bound).astype(held_as)


def bell_draw_with(stream_key, dims, width, most, shards, heavy, held_as=jnp.bfloat16):
    values = width * jax.random.normal(stream_key, dims, jnp.float32)
    if shards:
        values = values * level_of(stream_key, dims, shards, -0.22, 0.18)
    return jnp.clip(spiked(values, jax.random.fold_in(stream_key, 3), *heavy), -most, most).astype(held_as)


def setup_inputs(seed: int = 0) -> dict:
    key_list = jax.random.split(jax.random.key(seed), 7)
    return {
        "queries": draw_queries(jax.random.fold_in(key_list[6], 71), 0),
        "keys": draw_keys(jax.random.fold_in(key_list[6], 71), 0),
        "values": scatter_about(key_list[2], (TOKENS, D), 1.0, 6.0, ((0, 32), (1, 4))),
        "out_weight": scatter_about(key_list[3], (D, D), D ** -0.5, 0.1875, ((0, 4),)),
        "grad_output": bell_draw_with(key_list[4], (TOKENS, D), 1.0, 6.0, ((0, 32),), (0, 1, 32, 2.75)),
        "tile_lists": draw_tile_lists(jax.random.fold_in(key_list[6], 71), 0),
    }


def unfold_order(stored, span_len):
    pieces = stored.reshape((N_TM, 2, span_len) + stored.shape[1:])
    return jnp.concatenate([pieces[:, 0], pieces[::-1, 1]], axis=0)


def fold_order(ordered):
    stacked = jnp.stack([ordered[:N_TM], ordered[N_TM:][::-1]], axis=1)
    return stacked.reshape((-1,) + ordered.shape[2:])


def reference(queries, keys, values, out_weight, grad_output, tile_lists):
    score_scale = HD ** -0.5
    piece_count = 2 * N_TM
    q_seq = unfold_order(queries, STRETCH).reshape(piece_count, STRETCH, HEADS, HD)
    k_seq = unfold_order(keys, STRETCH).reshape(piece_count, STRETCH, HEADS, HD)
    v_seq = unfold_order(values, STRETCH).reshape(piece_count, STRETCH, HEADS, HD)
    list_seq = unfold_order(tile_lists, CT)
    zero_piece = jnp.zeros((1, STRETCH, HEADS, HD), queries.dtype)
    k_padded = jnp.concatenate([zero_piece, k_seq], axis=0)
    v_padded = jnp.concatenate([zero_piece, v_seq], axis=0)
    piece_ids = jnp.arange(piece_count, dtype=jnp.int32)

    def window_mask(piece_id):
        tile_rows = list_seq[piece_id]
        wanted = (piece_id - 1) * CT + jnp.arange(2 * CT, dtype=jnp.int32)
        matched = (tile_rows[:, :, None] == wanted[None, None, :]) & (tile_rows[:, :, None] >= 0)
        allow_tiles = jnp.any(matched, axis=1)
        allow_tiles = jnp.repeat(jnp.repeat(allow_tiles, QB, axis=0), QB, axis=1)
        causal = jnp.arange(2 * STRETCH)[None, :] <= jnp.arange(STRETCH)[:, None] + STRETCH
        return allow_tiles & causal

    def window_keys(piece_id):
        k_here = jnp.concatenate([k_padded[piece_id], k_padded[piece_id + 1]], axis=0).astype(jnp.float32)
        v_here = jnp.concatenate([v_padded[piece_id], v_padded[piece_id + 1]], axis=0).astype(jnp.float32)
        return k_here, v_here

    def logits_of(piece_id, k_here):
        q_here = q_seq[piece_id].astype(jnp.float32)
        logits = jnp.einsum('qhd,khd->hqk', q_here, k_here) * score_scale
        return jnp.where(window_mask(piece_id)[None], logits, -1e30)

    def forward_piece(piece_id):
        k_here, v_here = window_keys(piece_id)
        logits = logits_of(piece_id, k_here)
        row_max = jnp.max(logits, axis=-1, keepdims=True)
        probability = jnp.exp(logits - row_max)
        row_total = jnp.sum(probability, axis=-1, keepdims=True)
        prob_round = lax.optimization_barrier(probability.astype(jnp.bfloat16)).astype(jnp.float32)
        mixture = jnp.einsum('hqk,khd->qhd', prob_round, v_here)
        attended = (mixture / jnp.transpose(row_total, (1, 0, 2))).astype(jnp.bfloat16)
        return attended, row_max[..., 0] + jnp.log(row_total[..., 0])

    attended_seq, log_totals = lax.map(forward_piece, piece_ids)
    attended = fold_order(attended_seq.reshape(piece_count, STRETCH, D))
    output = jnp.dot(attended, out_weight, preferred_element_type=jnp.float32).astype(jnp.bfloat16)
    grad_attn = jnp.dot(grad_output, out_weight.T, preferred_element_type=jnp.float32).astype(jnp.bfloat16)
    grad_weight = jnp.dot(attended.T, grad_output, preferred_element_type=jnp.float32) * (TOKENS ** -0.5)
    g_seq = unfold_order(grad_attn, STRETCH).reshape(piece_count, STRETCH, HEADS, HD)
    row_delta = jnp.sum(g_seq.astype(jnp.float32) * attended_seq.astype(jnp.float32), axis=-1)

    def backward_piece(piece_id):
        k_here, v_here = window_keys(piece_id)
        logits = logits_of(piece_id, k_here)
        back_prob = jnp.exp(logits - log_totals[piece_id][..., None])
        back_round = lax.optimization_barrier(back_prob.astype(jnp.bfloat16)).astype(jnp.float32)
        g_here = g_seq[piece_id].astype(jnp.float32)
        q_here = q_seq[piece_id].astype(jnp.float32)
        dv_part = jnp.einsum('hqk,qhd->khd', back_round, g_here)
        dprob = jnp.einsum('qhd,khd->hqk', g_here, v_here)
        dscore = back_prob * (dprob - jnp.transpose(row_delta[piece_id])[:, :, None])
        dscore_round = lax.optimization_barrier(dscore.astype(jnp.bfloat16)).astype(jnp.float32)
        dq_here = (jnp.einsum('hqk,khd->qhd', dscore_round, k_here) * score_scale).astype(jnp.bfloat16)
        dk_part = jnp.einsum('hqk,qhd->khd', dscore_round, q_here) * score_scale
        return dq_here, dk_part, dv_part

    dq_seq, dk_parts, dv_parts = lax.map(backward_piece, piece_ids)

    def combine(parts):
        after = jnp.concatenate([parts[1:, :STRETCH], jnp.zeros_like(parts[:1, :STRETCH])], axis=0)
        summed = (parts[:, STRETCH:] + after).astype(jnp.bfloat16)
        return fold_order(summed.reshape(piece_count, STRETCH, D))

    grad_queries = fold_order(dq_seq.reshape(piece_count, STRETCH, D))
    grad_keys = combine(dk_parts)
    grad_values = combine(dv_parts)
    return output, grad_queries, grad_keys, grad_values, grad_weight
```

```python
import functools

import jax
import jax.numpy as jnp
from jax import lax
from jax.experimental import pallas as pl
from jax.experimental.pallas import tpu as pltpu
from jax.sharding import PartitionSpec as P

HD = 64
QB = 128
REACH = 5
NEG = -1e30


def dot(a, b, ca, cb):
    return lax.dot_general(a, b, (((ca,), (cb,)), ((), ())), preferred_element_type=jnp.float32)


def attention_kernel(
    allow_ref, flag_ref, q_ref, k_ref, v_ref, kvp_ref, kl_ref, vl_ref, g_ref,
    att_ref, dq_ref, dkvp_ref, dko_ref, dvo_ref,
    kwin, vwin, kt, vt, dk, dv, *, high,
):
    span, width = q_ref.shape
    heads = width // HD
    tiles = span // QB
    reach = REACH * QB
    if high:
        last = flag_ref[0] > 0

        @pl.when(last)
        def _():
            kwin[:span] = kl_ref[...]
            vwin[:span] = vl_ref[...]

        @pl.when(jnp.logical_not(last))
        def _():
            kwin[:span] = kvp_ref[:span]
            vwin[:span] = kvp_ref[span:]
    else:
        kwin[:span] = kvp_ref[:span]
        vwin[:span] = kvp_ref[span:]
    kwin[span:] = k_ref[...]
    vwin[span:] = v_ref[...]
    kt[...] = kwin[...].T
    vt[...] = vwin[...].T
    dk[...] = jnp.zeros_like(dk)
    dv[...] = jnp.zeros_like(dv)
    head_of = lax.broadcasted_iota(jnp.int32, (1, width), 1) // HD
    head_masks = [(head_of == h).astype(jnp.float32) for h in range(heads)]
    key_row = lax.broadcasted_iota(jnp.int32, (QB, heads * QB), 0)
    query_col = lax.broadcasted_iota(jnp.int32, (QB, heads * QB), 1) % QB
    causal = jnp.where(key_row <= query_col, 0.0, NEG)

    def stacked(x):
        return jnp.concatenate([(x * m).astype(jnp.bfloat16) for m in head_masks], axis=0)

    for t in range(tiles):
        rows = slice(t * QB, (t + 1) * QB)
        win = slice(t * QB, t * QB + reach)
        q_stack = stacked(q_ref[rows].astype(jnp.float32) * (HD ** -0.5))
        g_tile = g_ref[rows].astype(jnp.float32)
        g_stack = stacked(g_tile)
        g_t = g_tile.T
        s = dot(kwin[win], q_stack, 1, 1)
        blocks = []
        for j in range(REACH):
            bias = jnp.where(allow_ref[(tiles if high else 0) + t, j] > 0, 0.0, NEG)
            block = s[j * QB : (j + 1) * QB] + bias
            if j == REACH - 1:
                block = block + causal
            blocks.append(block)
        s = jnp.concatenate(blocks, axis=0)
        row_max = jnp.max(s, axis=0, keepdims=True)
        p = jnp.exp(s - row_max)
        total = jnp.sum(p, axis=0, keepdims=True)
        inv = 1.0 / total
        p_round = p.astype(jnp.bfloat16)
        att_parts = []
        delta_parts = []
        for h in range(heads):
            cols = slice(h * QB, (h + 1) * QB)
            feats = slice(h * HD, (h + 1) * HD)
            mix = dot(vt[feats, win], p_round[:, cols], 1, 0) * inv[:, cols]
            mix = mix.astype(jnp.bfloat16).astype(jnp.float32)
            att_parts.append(mix)
            delta_parts.append(jnp.sum(mix * g_t[feats], axis=0, keepdims=True))
        att_ref[rows] = jnp.concatenate(att_parts, axis=0).T.astype(jnp.bfloat16)
        delta = jnp.concatenate(delta_parts, axis=1)
        back = p * inv
        dv[win] += dot(back.astype(jnp.bfloat16), g_stack, 1, 0)
        dprob = dot(vwin[win], g_stack, 1, 1)
        ds = (back * (dprob - delta)).astype(jnp.bfloat16)
        dk[win] += dot(ds, q_stack, 1, 0)
        dq_parts = []
        for h in range(heads):
            cols = slice(h * QB, (h + 1) * QB)
            feats = slice(h * HD, (h + 1) * HD)
            dq_parts.append(dot(kt[feats, win], ds[:, cols], 1, 0))
        dq_ref[rows] = (jnp.concatenate(dq_parts, axis=0).T * (HD ** -0.5)).astype(jnp.bfloat16)
    dkvp_ref[:span] = dk[:span].astype(jnp.bfloat16)
    dkvp_ref[span:] = dv[:span].astype(jnp.bfloat16)
    dko_ref[...] = dk[span:]
    dvo_ref[...] = dv[span:]


def attention(allow, flag, queries, keys, values, kv_before, grad_attn, high):
    rows, width = queries.shape
    span = rows // 2
    half = 1 if high else 0
    own = pl.BlockSpec((span, width), lambda i: (half, 0))
    low = pl.BlockSpec((span, width), lambda i: (0, 0))
    both = pl.BlockSpec((2 * span, width), lambda i: (0, 0))
    smem = pl.BlockSpec(memory_space=pltpu.SMEM)
    return pl.pallas_call(
        functools.partial(attention_kernel, high=high),
        grid=(1,),
        in_specs=[smem, smem, own, own, own, both, low, low, own],
        out_specs=[low, low, both, low, low],
        out_shape=[
            jax.ShapeDtypeStruct((span, width), jnp.bfloat16),
            jax.ShapeDtypeStruct((span, width), jnp.bfloat16),
            jax.ShapeDtypeStruct((2 * span, width), jnp.bfloat16),
            jax.ShapeDtypeStruct((span, width), jnp.float32),
            jax.ShapeDtypeStruct((span, width), jnp.float32),
        ],
        scratch_shapes=[
            pltpu.VMEM((2 * span, width), jnp.bfloat16),
            pltpu.VMEM((2 * span, width), jnp.bfloat16),
            pltpu.VMEM((width, 2 * span), jnp.bfloat16),
            pltpu.VMEM((width, 2 * span), jnp.bfloat16),
            pltpu.VMEM((2 * span, width), jnp.float32),
            pltpu.VMEM((2 * span, width), jnp.float32),
        ],
        compiler_params=pltpu.CompilerParams(vmem_limit_bytes=48 * 1024 * 1024),
        name="attention_high" if high else "attention_low",
    )(allow, flag, queries, keys, values, kv_before, keys, values, grad_attn)


def output_kernel(*refs):
    out_ref = refs[-1]
    count = (len(refs) - 1) // 3
    weights = refs[2 * count : 3 * count]
    span = refs[0].shape[0]
    for half in range(2):
        parts = refs[half * count : (half + 1) * count]
        total = dot(parts[0][...], weights[0][...], 1, 0)
        for part, weight in zip(parts[1:], weights[1:]):
            total = total + dot(part[...], weight[...], 1, 0)
        out_ref[half * span : (half + 1) * span] = total.astype(jnp.bfloat16)


def shifted(x, by):
    devices = lax.axis_size("tm")
    return lax.ppermute(
        x, "tm", [(i, i + by) for i in range(devices) if 0 <= i + by < devices]
    )


def swapped(x, bit):
    devices = lax.axis_size("head")
    return lax.ppermute(x, "head", [(i, i ^ bit) for i in range(devices)])


def on_device(queries, keys, values, out_weight, grad_output, tile_lists):
    rows, width = queries.shape
    span = rows // 2
    tiles = span // QB
    tm_count = lax.axis_size("tm")
    tm_index = lax.axis_index("tm")
    head_index = lax.axis_index("head")
    is_last = tm_index == tm_count - 1
    token_total = tm_count * rows
    model = out_weight.shape[1]

    kv_low = shifted(jnp.concatenate([keys[:span], values[:span]], axis=0), 1)
    kv_high = shifted(jnp.concatenate([keys[span:], values[span:]], axis=0), -1)

    def weight_cols(head):
        return lax.dynamic_slice_in_dim(out_weight, head * width, width, axis=1)

    weights = [weight_cols(head_index)] + [
        swapped(weight_cols(head_index ^ bit), bit) for bit in (1, 2, 3)
    ]

    pieces = jnp.stack([tm_index, 2 * tm_count - 1 - tm_index])
    tile_ids = (pieces[:, None] * tiles + jnp.arange(tiles, dtype=jnp.int32)).reshape(-1)
    wanted = tile_ids[:, None] - (REACH - 1) + jnp.arange(REACH, dtype=jnp.int32)
    allow = jnp.any(
        (tile_lists[:, :, None] == wanted[:, None, :]) & (tile_lists[:, :, None] >= 0), axis=1
    ).astype(jnp.int32)
    flag = is_last.astype(jnp.int32).reshape(1)

    grad_attn = lax.dot_general(
        grad_output, out_weight, (((1,), (1,)), ((), ())), preferred_element_type=jnp.float32
    ).astype(jnp.bfloat16)

    gathered = []
    results = []
    for kv_before, high in ((kv_low, False), (kv_high, True)):
        att, dq, dkvp, dko, dvo = attention(
            allow, flag, queries, keys, values, kv_before, grad_attn, high
        )
        across = swapped(att, 2)
        gathered.append([att, swapped(att, 1), across, swapped(across, 1)])
        results.append((att, dq, dkvp, dko, dvo))
    (att_l, dq_l, dkvp_l, dko_l, dvo_l), (att_h, dq_h, dkvp_h, dko_h, dvo_h) = results
    back_low = shifted(dkvp_l, -1)
    back_high = shifted(dkvp_h, 1)

    attended = jnp.concatenate([att_l, att_h], axis=0)
    weight_term = lax.dot_general(
        grad_output, attended, (((0,), (0,)), ((), ())), preferred_element_type=jnp.float32
    ).astype(jnp.bfloat16)
    exchanged = lax.all_to_all(
        weight_term.reshape(tm_count, model // tm_count, width), "tm", 0, 0
    )
    grad_weight = (
        jnp.sum(exchanged.astype(jnp.float32), axis=0) * token_total ** (-0.5)
    ).T

    output = pl.pallas_call(
        output_kernel,
        out_shape=jax.ShapeDtypeStruct((rows, width), jnp.bfloat16),
        name="output",
    )(*gathered[0], *gathered[1], *weights)

    low_add = jnp.where(is_last, dkvp_h, back_low).astype(jnp.float32)
    high_add = back_high.astype(jnp.float32)
    grad_keys = jnp.concatenate([dko_l + low_add[:span], dko_h + high_add[:span]], axis=0)
    grad_values = jnp.concatenate([dvo_l + low_add[span:], dvo_h + high_add[span:]], axis=0)
    grad_queries = jnp.concatenate([dq_l, dq_h], axis=0)
    return (
        output,
        grad_queries,
        grad_keys.astype(jnp.bfloat16),
        grad_values.astype(jnp.bfloat16),
        grad_weight,
    )


def solution(mesh):
    return jax.shard_map(
        on_device,
        mesh=mesh,
        in_specs=(
            P("tm", "head"),
            P("tm", "head"),
            P("tm", "head"),
            P("head", None),
            P("tm", None),
            P("tm", None),
        ),
        out_specs=(
            P("tm", "head"),
            P("tm", "head"),
            P("tm", "head"),
            P("tm", "head"),
            P("head", "tm"),
        ),
        check_vma=False,
    )
```
